32 devices in a mesh: row: 4 (over x, core), col: 8 (over z, y).
Axes of the slice: x: 2, y: 2, z: 4, core: 2. Of those that a mesh axis runs over, the one named last changes fastest.
Arguments:
- hidden: bfloat16 [128, 8192], P('col', 'row'), may hold values from -6 to 6
- w_gate: bfloat16 [8192, 16384], P('row', 'col'), may hold values from -0.0625 to 0.0625
- w_up: bfloat16 [8192, 16384], P('row', 'col'), may hold values from -0.0625 to 0.0625
- prior: float32 [16384, 16384], P('row', 'col'), may hold values from -1 to 12, as said below
- rhs: float32 [16384, 4096], P('row', 'col'), may hold values from -6 to 6
Outputs:
- factored: float32 [16384, 16384], P('row', 'col')
- right_out: float32 [16384, 4096], P('row', 'col')
The draws below stay inside these ranges and needn't reach their ends.
Inputs may be any that keep to these rules, and one draw needn't show every extreme that they name: prior is symmetric and positive definite, with smallest eigenvalue 0.1 or more.
All inputs are finite; a program needn't handle non-finite values.
Results may differ from the reference program's by a relative error of at most 0.0003.
Values may be sent and summed in bfloat16 or wider, within the bound.
A program may use at most 192 MiB of HBM per device.

```python
import math
import jax
import jax.numpy as jnp
from jax import lax

D = 8192
KW = 16384
E = 4096
P_SIZE = 128
PANELS = 2
R = 128


def draw_prior(key, part):
    first = jax.random.fold_in(key, 11)
    second = jax.random.fold_in(key, 12)
    noise = jax.random.normal(first, (KW, KW), jnp.float32)
    base = (noise + noise.T) * (0.3 / math.sqrt(2.0 * KW))
    diagonal = jax.random.uniform(second, (KW,), jnp.float32, 1.0, 3.0)
    index = jnp.arange(KW, dtype=jnp.int32)
    base = base.at[index, index].add(diagonal)
    return base


def level_of(rng, shape, shards, smallest, largest):
    loudness = 1.0
    for axis_at, shards_of in shards:
        steps = jax.random.uniform(jax.random.fold_in(jax.random.fold_in(rng, 6), axis_at), (shards_of,), jnp.float32, smallest / len(shards), largest / len(shards))
        loudness = loudness * jnp.repeat(jnp.exp(steps), shape[axis_at] // shards_of).reshape((-1,) + (1,) * (len(shape) - 1 - axis_at))
    return loudness


def gaussian(rng, shape, width, reach, split=(), kind=jnp.bfloat16):
    array = jax.random.normal(rng, shape, jnp.float32) * width
    if len(split) > 0:
        array = level_of(rng, shape, split, -0.22, 0.18) * array
    return jnp.clip(array, min=-reach, max=reach).astype(kind)


def setup_inputs(seed: int = 0) -> dict:
    splits = jax.random.split(jax.random.key(seed), 6)
    return {
        "hidden": gaussian(splits[0], (R, D), 1.0, 6.0, ((0, 8), (1, 4))),
        "w_gate": gaussian(splits[1], (D, KW), D ** -0.5, 0.0625, ((0, 4), (1, 8))),
        "w_up": gaussian(splits[2], (D, KW), D ** -0.5, 0.0625, ((0, 4), (1, 8))),
        "prior": draw_prior(jax.random.fold_in(splits[5], 71), 0),
        "rhs": gaussian(splits[4], (KW, E), 1.0, 6.0, ((0, 4), (1, 8)), jnp.float32),
    }


DAMP = 0.5

def reference(hidden, w_gate, w_up, prior, rhs):
    gate = jnp.dot(hidden.astype(jnp.float32), w_gate.astype(jnp.float32), preferred_element_type=jnp.float32)
    upward = jnp.dot(hidden.astype(jnp.float32), w_up.astype(jnp.float32), preferred_element_type=jnp.float32)
    keys = jax.nn.silu(gate) * upward
    outer = jnp.dot(keys.T.astype(jnp.float32), keys.astype(jnp.float32), precision=lax.Precision.HIGHEST, preferred_element_type=jnp.float32)
    work = prior + outer / R
    index = jnp.arange(KW, dtype=jnp.int32)
    work = work.at[index, index].add(DAMP)
    right = rhs
    offsets = jnp.arange(P_SIZE, dtype=jnp.int32)
    below_diag = offsets[:, None] >= offsets[None, :]
    for panel in range(PANELS):
        start = panel * P_SIZE
        stop = start + P_SIZE
        pivot = jnp.linalg.cholesky(work[start:stop, start:stop])
        below = jax.scipy.linalg.solve_triangular(pivot, work[stop:, start:stop].T, lower=True).T
        solution = jax.scipy.linalg.solve_triangular(pivot, right[start:stop], lower=True)
        work = work.at[stop:, stop:].add(-jnp.dot(below.astype(jnp.float32), below.T.astype(jnp.float32), precision=lax.Precision.HIGHEST, preferred_element_type=jnp.float32))
        right = right.at[stop:].add(-jnp.dot(below.astype(jnp.float32), solution.astype(jnp.float32), precision=lax.Precision.HIGHEST, preferred_element_type=jnp.float32))
        right = right.at[start:stop].set(solution)
        block = jnp.where(below_diag, pivot, work[start:stop, start:stop])
        work = work.at[start:stop, start:stop].set(block)
        work = work.at[stop:, start:stop].set(below)
    return (work, right)
```

```python
import functools

import jax
import jax.numpy as jnp
from jax import lax
from jax.experimental import pallas as pl
from jax.experimental.pallas import tpu as pltpu
from jax.sharding import PartitionSpec as P

P_SIZE = 128
PANELS = 2
DAMP = 0.5
HIGH = lax.Precision.HIGHEST


def dot(a, b, dims=((1,), (0,))):
    return lax.dot_general(
        a, b, (dims, ((), ())), precision=HIGH, preferred_element_type=jnp.float32
    )


def split(value):
    high = lax.reduce_precision(value, 8, 7)
    return high.astype(jnp.bfloat16), (value - high).astype(jnp.bfloat16)


def eliminate(work, out):
    n = work.shape[0]
    lanes = lax.broadcasted_iota(jnp.int32, (n, n), 1)
    rows = lax.broadcasted_iota(jnp.int32, (n, 1), 0)

    def step(j, carry):
        row = work[pl.ds(j, 1), :]
        block = work[...]
        here = lanes == j
        column = jnp.sum(jnp.where(here, block[:, :n], 0.0), axis=1, keepdims=True)
        pivot = jnp.sum(jnp.where(here[:1], row[:, :n], 0.0), axis=1, keepdims=True)
        out[pl.ds(j, 1), :] = row / jnp.sqrt(pivot)
        work[...] = block - jnp.where(rows > j, column, 0.0) * (row / pivot)
        return carry

    lax.fori_loop(0, n, step, 0)


def inverse_kernel(a_ref, o_ref, work, out):
    size = a_ref.shape[0]
    n = P_SIZE
    eye = (
        lax.broadcasted_iota(jnp.int32, (n, n), 0)
        == lax.broadcasted_iota(jnp.int32, (n, n), 1)
    ).astype(jnp.float32)
    o_ref[...] = jnp.zeros_like(o_ref)
    for panel in range(size // n):
        c, e = panel * n, panel * n + n
        block = a_ref[c:e, c:e]
        if panel:
            left = dot(a_ref[c:e, :c], o_ref[:c, :c], ((1,), (1,)))
            block = block - dot(left, left, ((1,), (1,)))
        work[:, :n] = block
        work[:, n:] = eye
        eliminate(work, out)
        inverse = out[:, n:]
        o_ref[c:e, c:e] = inverse
        if panel:
            o_ref[c:e, :c] = -dot(inverse, dot(left, o_ref[:c, :c]))


def update_kernel(
    panels, at_ref, a_ref, b_ref, y_ref, yb_ref, factor_ref, prior_ref, rhs_ref, o_ref, r_ref
):
    tile, width = prior_ref.shape
    keyed = b_ref.shape[0] // 3 - panels
    row0 = at_ref[0] + pl.program_id(0) * tile
    col0 = at_ref[1]
    half = keyed + panels
    a = a_ref[...]
    high = a[:, half:]
    o_ref[...] = (
        prior_ref[...]
        + jnp.dot(a, b_ref[: 2 * half], preferred_element_type=jnp.float32)
        + jnp.dot(high, b_ref[2 * half :], preferred_element_type=jnp.float32)
    )
    r_ref[...] = (
        rhs_ref[...]
        + jnp.dot(a[:, keyed:half], yb_ref[:panels], preferred_element_type=jnp.float32)
        + jnp.dot(high[:, keyed:], yb_ref[:panels], preferred_element_type=jnp.float32)
        + jnp.dot(high[:, keyed:], yb_ref[panels:], preferred_element_type=jnp.float32)
    )

    @pl.when((row0 < col0 + width) & (col0 < row0 + tile))
    def _():
        start = pl.multiple_of(jnp.clip(row0 - col0, 0, width - tile), 128)
        rows = row0 + lax.broadcasted_iota(jnp.int32, (tile, tile), 0)
        cols = col0 + start + lax.broadcasted_iota(jnp.int32, (tile, tile), 1)
        there = o_ref[:, pl.ds(start, tile)]
        o_ref[:, pl.ds(start, tile)] = there + jnp.where(rows == cols, DAMP, 0.0)

    @pl.when(col0 == 0)
    def _():
        rows = row0 + lax.broadcasted_iota(jnp.int32, (tile, panels), 0)
        cols = lax.broadcasted_iota(jnp.int32, (tile, panels), 1)
        o_ref[:, :panels] = jnp.where(rows >= cols, factor_ref[...], o_ref[:, :panels])

    @pl.when(row0 == 0)
    def _():
        r_ref[:panels, :] = y_ref[...]


def local(hidden, w_gate, w_up, prior, rhs):
    rows_count = lax.axis_size("row")
    cols_count = lax.axis_size("col")
    row_id = lax.axis_index("row")
    col_id = lax.axis_index("col")
    ratio = cols_count // rows_count
    height, width = prior.shape
    wide = PANELS * P_SIZE
    columns = rhs.shape[1]
    first_row, first_col = row_id == 0, col_id == 0

    tokens = lax.all_gather(hidden, "col", axis=0, tiled=True)
    samples = tokens.shape[0]
    gate_part = jnp.dot(tokens, w_gate, preferred_element_type=jnp.float32)
    up_part = jnp.dot(tokens, w_up, preferred_element_type=jnp.float32)

    def keys_of(gate, up):
        return jax.nn.silu(gate) * up

    corner = jnp.where(first_row & first_col, prior[:wide, :wide], 0.0)
    pivots = jnp.concatenate([gate_part[:, :wide], up_part[:, :wide]], axis=0)
    pivots = jnp.concatenate([jnp.where(first_col, pivots, 0.0), corner], axis=0)
    pivots = lax.psum(pivots, ("row", "col"))
    pivot_keys = keys_of(pivots[:samples], pivots[samples : 2 * samples])
    index = lax.iota(jnp.int32, wide)
    eye = (index[:, None] == index[None, :]).astype(jnp.float32)
    pivot = (
        pivots[2 * samples :]
        + dot(pivot_keys, pivot_keys, ((0,), (0,))) / samples
        + DAMP * eye
    )
    inverse = pl.pallas_call(
        inverse_kernel,
        out_shape=jax.ShapeDtypeStruct((wide, wide), jnp.float32),
        scratch_shapes=[pltpu.VMEM((P_SIZE, 2 * P_SIZE), jnp.float32)] * 2,
    )(pivot)

    parts = jnp.stack([gate_part, up_part])
    parts = lax.psum_scatter(parts, "row", scatter_dimension=2, tiled=True)
    part_keys = keys_of(parts[0], parts[1])
    keys = lax.all_gather(part_keys, "row", axis=1, tiled=True)
    moves = [
        (r * cols_count + c, (c // ratio) * cols_count + (c % ratio) * rows_count + r)
        for r in range(rows_count)
        for c in range(cols_count)
    ]
    moved = lax.ppermute(part_keys, ("row", "col"), moves)
    row_keys_t = lax.all_gather(moved.T, "col", axis=0, tiled=True)

    late = part_keys[0, 0] * 0.0
    narrow = prior.at[:, :wide].get()
    prior_rows = jnp.where(first_col, narrow, 0.0).astype(jnp.bfloat16)
    prior_cols = jnp.where(first_row, prior[:wide], 0.0).astype(jnp.bfloat16)
    top = jnp.where(first_row, rhs[:wide], 0.0)
    prior_rows, prior_cols, top, _ = lax.optimization_barrier(
        (prior_rows, prior_cols, top, late)
    )
    prior_rows = lax.psum(prior_rows, "col").astype(jnp.float32)
    prior_cols = lax.psum(prior_cols, "row").astype(jnp.float32)
    top = lax.psum(top, "row")
    prior_rows = jnp.where(first_col, narrow, prior_rows)

    panel_rows = prior_rows + dot(row_keys_t, pivot_keys) / samples
    row_global = row_id * height + lax.iota(jnp.int32, height)
    col_global = col_id * width + lax.iota(jnp.int32, width)
    panel_rows = panel_rows + jnp.where(row_global[:, None] == index[None, :], DAMP, 0.0)
    factor_rows = dot(panel_rows, inverse, ((1,), (1,)))
    panel_cols = prior_cols + dot(pivot_keys, keys, ((0,), (0,))) / samples
    factor_cols = dot(inverse, panel_cols)
    solved = dot(inverse, top)

    stops = (index // P_SIZE + 1) * P_SIZE
    lower = jnp.where(row_global[:, None] >= stops[None, :], -factor_rows, 0.0)
    upper = jnp.where(col_global[None, :] >= stops[:, None], factor_cols, 0.0)
    rk_high, rk_low = split(row_keys_t)
    lo_high, lo_low = split(lower)
    ck_high, ck_low = split(keys / samples)
    up_high, up_low = split(upper)
    left = jnp.concatenate([rk_low, lo_low, rk_high, lo_high], axis=1)
    right = jnp.concatenate([ck_high, up_high, ck_high, up_high, ck_low, up_low], axis=0)
    solved_parts = jnp.concatenate(split(solved), axis=0)
    at = jnp.stack([row_id * height, col_id * width]).astype(jnp.int32)

    tile = min(512, height, width)
    by_row = lambda i, at: (i, 0)
    whole = lambda i, at: (0, 0)
    once = pl.Buffered(1)
    return pl.pallas_call(
        functools.partial(update_kernel, wide),
        grid_spec=pltpu.PrefetchScalarGridSpec(
            num_scalar_prefetch=1,
            grid=(height // tile,),
            in_specs=[
                pl.BlockSpec((tile, left.shape[1]), by_row),
                pl.BlockSpec(right.shape, whole, pipeline_mode=once),
                pl.BlockSpec(solved.shape, whole, pipeline_mode=once),
                pl.BlockSpec(solved_parts.shape, whole, pipeline_mode=once),
                pl.BlockSpec((tile, wide), by_row),
                pl.BlockSpec((tile, width), by_row),
                pl.BlockSpec((tile, columns), by_row),
            ],
            out_specs=[
                pl.BlockSpec((tile, width), by_row),
                pl.BlockSpec((tile, columns), by_row),
            ],
        ),
        out_shape=(
            jax.ShapeDtypeStruct(prior.shape, jnp.float32),
            jax.ShapeDtypeStruct(rhs.shape, jnp.float32),
        ),
        compiler_params=pltpu.CompilerParams(dimension_semantics=("arbitrary",)),
    )(at, left, right, solved, solved_parts, factor_rows, prior, rhs)


def solution(mesh):
    return jax.shard_map(
        local,
        mesh=mesh,
        in_specs=(
            P("col", "row"),
            P("row", "col"),
            P("row", "col"),
            P("row", "col"),
            P("row", "col"),
        ),
        out_specs=(P("row", "col"), P("row", "col")),
        check_vma=False,
    )
```
